32 devices in a mesh: ox: 4 (over y, core), oy: 8 (over z, x).
Axes of the slice: x: 2, y: 2, z: 4, core: 2. Of those that a mesh axis runs over, the one named last changes fastest.
Arguments:
- ocean_state: bfloat16 [512, 720, 256], P('oy', 'ox'), may hold values from -6 to 6
- diffusivity: float32 [512, 720], P('oy', 'ox'), may hold values from 0.04 to 0.24
- requests: int32 [32, 32, 2], P(('ox', 'oy')), may hold values from 0 to 89
- slot_ids: int32 [768, 16], P(('ox', 'oy')), may hold values from 0 to 63
- counts: int32 [768], P(('ox', 'oy')), may hold values from 1 to 16, as said below
- remap_weights: bfloat16 [768, 16, 128, 128], P(('ox', 'oy')), may hold values from -0.125 to 0.125
Outputs:
- atmosphere: bfloat16 [768, 128, 256], P(('ox', 'oy'))
The draws below stay inside these ranges and needn't reach their ends.
Inputs may be any that keep to these rules, and one draw needn't show every extreme that they name: `counts`: at most 16; exactly 16 for some destination block in every draw.
All inputs are finite; a program needn't handle non-finite values.
Results may differ from the reference program's by a relative error of at most 0.0049.
Values may be sent and summed in bfloat16 or wider, within the bound.
No kernel may reach another device: no remote copies, remote signals or barrier semaphores. Data moves between devices by JAX's collectives and lax.ppermute only.
A program may use at most 128 MiB of HBM per device.

```python
import math
import jax
import jax.numpy as jnp
from jax import lax

CH = 256
COLS = 180
ROWS = 64
BLOCK = 128
SRC_DEV = 90
DST_DEV = 24
KMAX = 16
CAP = 2
NY = 512
NX = 720
NDST = 768
N_OX = 4
N_OY = 8
DEVICES = 32


def draw_counts(key, part):
    dest_count = DST_DEV * DEVICES
    position = jnp.arange(dest_count, dtype=jnp.int32)
    tile_row = position // DST_DEV % N_OY
    crowded = tile_row >= N_OY - max(1, N_OY // 4)
    ceiling = jnp.where(crowded, KMAX, max(1, KMAX // 4))
    drawn = jax.random.randint(jax.random.fold_in(key, 11), (dest_count,), 0, 1 << 20)
    values = drawn % ceiling + 1
    leading = position % DST_DEV == 0
    return jnp.where(crowded & leading, KMAX, values).astype(jnp.int32)


def with_ends(array, own_key, least, top_value):
    place = [jax.random.randint(jax.random.fold_in(own_key, axis), (), 0, length) for axis, length in enumerate(array.shape)]
    widest = array.shape.index(max(array.shape))
    next_to = place[:widest] + [(place[widest] + 1) % array.shape[widest]] + place[widest + 1:]
    return array.at[tuple(place)].set(least).at[tuple(next_to)].set(top_value)


def levels(rng, shape, pieces, smallest, top_value):
    gain = 1.0
    for axis_at, blocks in pieces:
        steps = jax.random.uniform(jax.random.fold_in(jax.random.fold_in(rng, 6), axis_at), (blocks,), jnp.float32, smallest / len(pieces), top_value / len(pieces))
        gain = gain * jnp.repeat(jnp.exp(steps), shape[axis_at] // blocks).reshape((-1,) + (1,) * (len(shape) - 1 - axis_at))
    return gain


def bell_draw(own_key, extent, scale, limit, split=(), kind=jnp.bfloat16):
    level = levels(own_key, extent, split, -0.22, 0.18) if split else 1.0
    values = jax.random.normal(own_key, extent, jnp.float32) * scale * level
    return jnp.minimum(jnp.maximum(values, -limit), limit).astype(kind)


def setup_inputs(seed: int = 0) -> dict:
    splits = jax.random.split(jax.random.key(seed), 7)
    return {
        "ocean_state": bell_draw(splits[0], (NY, NX, CH), 1.0, 6.0, ((0, 8), (1, 4))),
        "diffusivity": jnp.clip(jnp.exp(math.log(0.24) - 1.7917595 * jax.random.uniform(splits[1], (NY, NX), jnp.float32) ** levels(splits[1], (NY, NX), ((0, 8), (1, 4)), -0.2, 0.2)), 0.04, 0.24),
        "requests": with_ends(jax.random.randint(splits[2], (DEVICES, DEVICES, CAP), 0, SRC_DEV), jax.random.fold_in(splits[2], 1), 0, SRC_DEV - 1).astype(jnp.int32),
        "slot_ids": with_ends(jax.random.randint(splits[3], (NDST, KMAX), 0, DEVICES * CAP), jax.random.fold_in(splits[3], 1), 0, (DEVICES * CAP) - 1).astype(jnp.int32),
        "counts": draw_counts(jax.random.fold_in(splits[6], 71), 0),
        "remap_weights": bell_draw(splits[5], (NDST, KMAX, BLOCK, BLOCK), (BLOCK * KMAX) ** -0.5, 0.125, ((0, 32),)),
    }


def smooth_strip(padded, diffusivity, start):
    window = lax.dynamic_slice_in_dim(padded, start, ROWS + 2, 0).astype(jnp.float32)
    centre = window[1:-1]
    coeff = lax.dynamic_slice_in_dim(diffusivity, start, ROWS, 0)[:, :, None]
    beside = window[2:] + window[:-2] + jnp.roll(centre, -1, axis=1) + jnp.roll(centre, 1, axis=1)
    return (centre + coeff * (beside - 4.0 * centre)).astype(jnp.bfloat16)


def reference(ocean_state, diffusivity, requests, slot_ids, counts, remap_weights):
    bottom = jnp.zeros((1, NX, CH), jnp.bfloat16)
    padded = jnp.concatenate([bottom, ocean_state, ocean_state[-1:, ::-1]], 0)
    starts = jnp.arange(N_OY, dtype=jnp.int32) * ROWS
    strips = lax.map(lambda start: smooth_strip(padded, diffusivity, start), starts)
    blocks = strips.reshape(N_OY, ROWS, N_OX, COLS, CH).transpose(2, 0, 1, 3, 4)
    blocks = blocks.reshape(N_OX * N_OY * SRC_DEV, BLOCK, CH)
    tiles = (jnp.arange(NDST, dtype=jnp.int32) // DST_DEV).astype(jnp.int32)
    source = slot_ids // CAP
    column = slot_ids % CAP
    local_ids = requests[tiles[:, None], source, column]
    ident = (source * SRC_DEV + local_ids).astype(jnp.int32)
    live_mask = jnp.arange(KMAX, dtype=jnp.int32)[None, :] < counts[:, None]
    tile_count = N_OX * N_OY

    def one_tile(packed):
        weights, idents, mask = packed
        picked = blocks[idents].astype(jnp.float32)
        scaled = weights.astype(jnp.float32) * mask[:, :, None, None].astype(jnp.float32)
        summed = jnp.einsum("dkij,dkjc->dic", scaled, picked)
        return summed.astype(jnp.bfloat16)

    result = lax.map(one_tile, (remap_weights.reshape(tile_count, DST_DEV, KMAX, BLOCK, BLOCK),
                                ident.reshape(tile_count, DST_DEV, KMAX),
                                live_mask.reshape(tile_count, DST_DEV, KMAX)))
    return result.reshape(NDST, BLOCK, CH)
```

```python
import functools

import jax
import jax.numpy as jnp
from jax import lax
from jax.experimental import pallas as pl
from jax.experimental.pallas import tpu as pltpu
from jax.sharding import PartitionSpec as P

BLOCK = 128
LANES = 128
PACK = 16
AXES = ("ox", "oy")


def flatten_kernel(field_ref, out_ref, wide, rows32):
    columns, rows, channels = field_ref.shape
    pitch = wide.shape[1] // columns

    @pl.loop(0, columns, unroll=4)
    def _(column):
        value = field_ref[column].astype(jnp.float32)
        for half in range(channels // LANES):
            part = value[:, half * LANES : (half + 1) * LANES]
            wide[half, pl.ds(column * pitch, rows), :] = part

    for row in range(rows):
        for half in range(channels // LANES):
            picked = wide[half, pl.ds(row, columns, stride=pitch), :]
            rows32[half, pl.ds(row * columns, columns), :] = picked

    @pl.loop(0, rows * columns // PACK, unroll=4)
    def _(step):
        base = pl.multiple_of(step * PACK, PACK)
        halves = [rows32[half, pl.ds(base, PACK), :] for half in range(channels // LANES)]
        out_ref[step] = jnp.concatenate(halves, 1).astype(out_ref.dtype)


def flatten_cells(field):
    columns, rows, channels = field.shape
    pieces = rows // PACK
    size = columns * PACK // PACK
    return pl.pallas_call(
        flatten_kernel,
        out_shape=jax.ShapeDtypeStruct(((pieces + 2) * size, PACK, channels), field.dtype),
        grid=(pieces,),
        in_specs=[pl.BlockSpec((columns, PACK, channels), lambda i: (0, i, 0))],
        out_specs=pl.BlockSpec((size, PACK, channels), lambda i: (i + 1, 0, 0)),
        scratch_shapes=[
            pltpu.VMEM((channels // LANES, columns * (PACK + 1), LANES), jnp.float32),
            pltpu.VMEM((channels // LANES, columns * PACK, LANES), jnp.float32),
        ],
        cost_estimate=pl.CostEstimate(flops=0, bytes_accessed=24 << 20, transcendentals=0),
        name="flatten",
    )(field)


def smooth_kernel(masks, columns, rows, cap, asked, place, cells, coeff_ref, east_ref, west_ref, south_ref, north_ref, *rest):
    outs = rest[: len(masks)]
    mid, top, bot, mid32, top32, bot32, rim_e, rim_w, rim_s, rim_n, made, in_sem, out_sem = rest[len(masks) :]
    channels = east_ref.shape[1]
    halves = channels // LANES
    me = place[0]
    up, shift = columns // PACK, columns % PACK
    parts = ((mid, -1, mid32), (top, up, top32), (bot, -up - 1, bot32))

    def request(i):
        mask = masks[0]
        for j in range(1, len(masks)):
            mask = jnp.where(i // cap == j, masks[j], mask)
        return asked[me ^ mask, i % cap]

    def fetch(i):
        start = columns + request(i) * (BLOCK // PACK)
        return [
            pltpu.make_async_copy(cells.at[pl.ds(start + offset, ref.shape[1])], ref.at[i], in_sem.at[i])
            for ref, offset, _ in parts
        ]

    @pl.loop(0, len(masks) * cap)
    def _(i):
        for copy in fetch(i):
            copy.start()

    for half in range(halves):
        lanes = pl.ds(half * LANES, LANES)
        rim_e[half] = east_ref[:, lanes].astype(jnp.float32)
        rim_w[half] = west_ref[:, lanes].astype(jnp.float32)
        rim_s[half] = south_ref[:, lanes].astype(jnp.float32)
        rim_n[half] = north_ref[:, lanes].astype(jnp.float32)
    cell = lax.broadcasted_iota(jnp.int32, (BLOCK, LANES), 0)

    @pl.loop(0, len(masks) * cap)
    def _(i):
        for copy in fetch(i):
            copy.wait()
        for ref, _, wide in parts:
            for step in range(ref.shape[1]):
                value = ref[i, step].astype(jnp.float32)
                for half in range(halves):
                    part = value[:, half * LANES : (half + 1) * LANES]
                    wide[half, step * PACK : (step + 1) * PACK, :] = part
        block = request(i)
        total = rows * columns // BLOCK
        for c in range(pl.cdiv(columns, BLOCK)):
            low = c * BLOCK
            size = min(BLOCK, columns - low)

            @pl.when(block == c)
            def _():
                for half in range(halves):
                    bot32[half, PACK - shift : PACK - shift + size, :] = rim_s[half, low : low + size, :]

            begin = (total - 1 - c) * BLOCK - (rows - 1) * columns
            skip = max(0, -begin)

            @pl.when(block == total - 1 - c)
            def _():
                for half in range(halves):
                    top32[half, shift + skip : shift + BLOCK, :] = rim_n[half, begin + skip : begin + BLOCK, :]

        row = (block * BLOCK + columns - 1) // columns
        edge = row * columns - block * BLOCK
        row_w = jnp.minimum(row, rows - 1)
        row_e = jnp.maximum(row - 1, 0)
        scale = jnp.broadcast_to(coeff_ref[pl.ds(block, 1), :], (BLOCK, LANES)).T
        for half in range(halves):
            centre = mid32[half, PACK : PACK + BLOCK, :]
            east = mid32[half, PACK + 1 : PACK + 1 + BLOCK, :]
            west = mid32[half, PACK - 1 : PACK - 1 + BLOCK, :]
            north = top32[half, shift : shift + BLOCK, :]
            south = bot32[half, PACK - shift : PACK - shift + BLOCK, :]
            west = jnp.where(cell == edge, rim_w[half, pl.ds(row_w, 1), :], west)
            east = jnp.where(cell == edge - 1, rim_e[half, pl.ds(row_e, 1), :], east)
            beside = north + south + east + west
            value = centre + scale * (beside - 4.0 * centre)
            made[i, :, half * LANES : (half + 1) * LANES] = value.astype(made.dtype)

    sends = []
    for j, out in enumerate(outs):
        sends.append(pltpu.make_async_copy(made.at[pl.ds(j * cap, cap)], out, out_sem.at[j]))
        sends[-1].start()
    for send in sends:
        send.wait()


def smooth_blocks(masks, asked, place, cells, coeff, east, west, south, north):
    channels = cells.shape[2]
    cap = asked.shape[1]
    count = len(masks) * cap
    run = BLOCK // PACK
    rows, columns = east.shape[0], south.shape[0]
    anywhere = pl.BlockSpec(memory_space=pl.ANY)
    inside = pl.BlockSpec(memory_space=pltpu.VMEM)
    steps = (run + 2, run + 1, run + 1)
    halves = channels // LANES
    return pl.pallas_call(
        functools.partial(smooth_kernel, masks, columns, rows, cap),
        out_shape=[jax.ShapeDtypeStruct((cap, BLOCK, channels), cells.dtype)] * len(masks),
        grid_spec=pltpu.PrefetchScalarGridSpec(
            num_scalar_prefetch=2,
            grid=(),
            in_specs=[anywhere] + [inside] * 5,
            out_specs=[anywhere] * len(masks),
            scratch_shapes=[pltpu.VMEM((count, n, PACK, channels), cells.dtype) for n in steps]
            + [pltpu.VMEM((halves, n * PACK, LANES), jnp.float32) for n in steps]
            + [pltpu.VMEM((halves, n, LANES), jnp.float32) for n in (rows, rows, columns, columns)]
            + [
                pltpu.VMEM((count, BLOCK, channels), cells.dtype),
                pltpu.SemaphoreType.DMA((count,)),
                pltpu.SemaphoreType.DMA((len(masks),)),
            ],
        ),
        cost_estimate=pl.CostEstimate(
            flops=count * BLOCK * channels * 8,
            bytes_accessed=count * BLOCK * channels * 10,
            transcendentals=0,
        ),
        name="smooth",
    )(asked, place, cells, coeff, east, west, south, north)


def remap_kernel(masks, cap, slots, has_start, table, weights, *rest):
    arrived = rest[: len(masks)]
    rest = rest[len(masks) :]
    start_ref = rest[0] if has_start else None
    out_ref, blocks, held, block_sem, weight_sem = rest[1 if has_start else 0 :]
    dests, terms = held.shape[:2]
    per_step = out_ref.shape[0]
    step = pl.program_id(0)
    me = table[0, terms + 1]

    sizes = [size for size in (4, 8) if size < terms] + [terms]

    def used(dest):
        number = table[dest, terms]
        size = jnp.int32(terms)
        for bound in sizes[-2::-1]:
            size = jnp.where(number <= bound, bound, size)
        return jnp.where(number > 0, size, 0)

    def weight_copy(dest, place):
        term = table[dest, place] // 65536
        return pltpu.make_async_copy(weights.at[dest, term], held.at[dest, place], weight_sem.at[dest])

    def block_copy(j):
        where = pl.ds((me ^ masks[j]) * cap, cap)
        return pltpu.make_async_copy(arrived[j], blocks.at[where], block_sem.at[j])

    @pl.when(step == 0)
    def _():
        for j in range(len(masks)):
            block_copy(j).start()

        @pl.loop(0, dests)
        def _(dest):
            @pl.loop(0, used(dest))
            def _(place):
                weight_copy(dest, place).start()

        blocks[slots] = jnp.zeros(blocks.shape[1:], blocks.dtype)
        for j in range(len(masks)):
            block_copy(j).wait()

    def product(dest, size):
        left = [held[dest, g] for g in range(size)]
        right = [blocks[table[dest, g] % 65536] for g in range(size)]
        return jnp.dot(
            jnp.concatenate(left, 1), jnp.concatenate(right, 0), preferred_element_type=jnp.float32
        )

    for u in range(per_step):
        dest = step * per_step + u

        @pl.loop(0, used(dest))
        def _(place):
            weight_copy(dest, place).wait()

    for u in range(per_step):
        dest = step * per_step + u
        size = used(dest)

        @pl.when(size == 0)
        def _():
            value = start_ref[u] if has_start else jnp.zeros(out_ref.shape[1:], jnp.float32)
            out_ref[u] = value.astype(out_ref.dtype)

        for bound in sizes:

            @pl.when(size == bound)
            def _():
                value = product(dest, bound)
                value = start_ref[u] + value if has_start else value
                out_ref[u] = value.astype(out_ref.dtype)


def remap(masks, cap, slots, table, weights, arrived, start, dtype):
    dests, terms = weights.shape[:2]
    channels = arrived[0].shape[2]
    per_step = 4 if dests % 4 == 0 else 1
    anywhere = pl.BlockSpec(memory_space=pl.ANY)
    tile = pl.BlockSpec((per_step, BLOCK, channels), lambda i, *_: (i, 0, 0))
    extra = [] if start is None else [start]
    return pl.pallas_call(
        functools.partial(remap_kernel, masks, cap, slots, start is not None),
        out_shape=jax.ShapeDtypeStruct((dests, BLOCK, channels), dtype),
        grid_spec=pltpu.PrefetchScalarGridSpec(
            num_scalar_prefetch=1,
            grid=(dests // per_step,),
            in_specs=[anywhere] * (1 + len(masks)) + [tile] * len(extra),
            out_specs=tile,
            scratch_shapes=[
                pltpu.VMEM((slots + 1, BLOCK, channels), arrived[0].dtype),
                pltpu.VMEM((dests, terms, BLOCK, BLOCK), weights.dtype),
                pltpu.SemaphoreType.DMA((len(masks),)),
                pltpu.SemaphoreType.DMA((dests,)),
            ],
        ),
        compiler_params=pltpu.CompilerParams(vmem_limit_bytes=48 << 20),
        cost_estimate=pl.CostEstimate(
            flops=dests * terms * BLOCK * BLOCK * channels,
            bytes_accessed=weights.size,
            transcendentals=0,
        ),
        name="remap",
    )(table, weights, *arrived, *extra)


def term_table(slot_ids, chosen, slots, me):
    terms = slot_ids.shape[1]
    index = jnp.arange(terms, dtype=jnp.int32)
    key = jnp.where(chosen, index[None, :], index[None, :] + terms)
    rank = jnp.sum(key[:, None, :] < key[:, :, None], axis=2)
    entry = index[None, :] * 65536 + jnp.where(chosen, slot_ids, slots)
    hit = rank[:, :, None] == index[None, None, :]
    ordered = jnp.sum(jnp.where(hit, entry[:, :, None], 0), axis=1)
    number = jnp.sum(chosen, axis=1, dtype=jnp.int32)[:, None]
    return jnp.concatenate([ordered, number, jnp.full_like(number, me)], axis=1)


def body(ocean_state, diffusivity, requests, slot_ids, counts, remap_weights):
    n_ox, n_oy = lax.axis_size("ox"), lax.axis_size("oy")
    devices = n_ox * n_oy
    rows, columns, channels = ocean_state.shape
    cap = requests.shape[2]
    slots = devices * cap
    ox, oy = lax.axis_index("ox"), lax.axis_index("oy")
    me = (ox * n_oy + oy).astype(jnp.int32)
    assert devices & (devices - 1) == 0 and n_oy % 2 == 0 and rows % PACK == 0

    asked = lax.all_to_all(requests[0], AXES, split_axis=0, concat_axis=0, tiled=True)
    field = jnp.transpose(ocean_state, (1, 0, 2))
    ring = [(i, (i + 1) % n_ox) for i in range(n_ox)]
    west = lax.ppermute(field[-1], "ox", ring)
    east = lax.ppermute(field[0], "ox", [(j, i) for i, j in ring])
    first_row, last_row = ocean_state[0], ocean_state[-1]
    odd = oy % 2 == 1
    top = n_oy - 1
    pairs = [(ox_ * n_oy + i, ox_ * n_oy + (i ^ 1)) for ox_ in range(n_ox) for i in range(n_oy)]
    inner = lax.ppermute(jnp.where(odd, first_row, last_row), AXES, pairs)
    pairs = [(i * n_oy + top, (n_ox - 1 - i) * n_oy + top) for i in range(n_ox)]
    for i in range(1, top, 2):
        for ox_ in range(n_ox):
            base = ox_ * n_oy + i
            pairs += [(base, base + 1), (base + 1, base)]
    outer = lax.ppermute(jnp.where(odd, last_row, first_row), AXES, pairs)
    north = jnp.where(oy == top, outer[::-1], jnp.where(odd, outer, inner))
    south = jnp.where(odd, inner, outer)

    cells = flatten_cells(field)
    coeff = diffusivity.reshape(-1, BLOCK)
    place = me[None]

    half = n_oy // 2
    across = [m for m in range(devices) if m & half]
    beside = [m for m in range(devices) if not m & half]
    order = []
    for a, b in zip(across, beside[1:] + [beside[0]]):
        order += [a, b]
    late = across[-len(across) // 8 :]
    order = [m for m in order if m not in late] + late
    groups = [order[:2], order[2:6]] + [order[i : i + 6] for i in range(6, devices, 6)]
    arrived = {}
    for group in groups:
        made = smooth_blocks(tuple(group), asked, place, cells, coeff, east, west, south, north)
        for m, blocks in zip(group, made):
            pairs = [(i, i ^ m) for i in range(devices)]
            arrived[m] = lax.ppermute(blocks, AXES, pairs) if m else blocks

    term_total = slot_ids.shape[1]
    live = jnp.arange(term_total, dtype=jnp.int32)[None, :] < counts[:, None]
    offset = me ^ (slot_ids // cap)
    is_late = functools.reduce(jnp.logical_or, [offset == m for m in late])
    early = [m for m in order if m not in late]
    table_1 = term_table(slot_ids, live & ~is_late, slots, me)
    table_2 = term_table(slot_ids, live & is_late, slots, me)
    partial = remap(
        tuple(early), cap, slots, table_1, remap_weights, [arrived[m] for m in early], None, jnp.float32
    )
    return remap(
        tuple(late), cap, slots, table_2, remap_weights, [arrived[m] for m in late], partial, jnp.bfloat16
    )


def solution(mesh):
    placed = (
        P("oy", "ox", None),
        P("oy", "ox"),
        P(("ox", "oy"), None, None),
        P(("ox", "oy"), None),
        P(("ox", "oy")),
        P(("ox", "oy"), None, None, None),
    )
    return jax.shard_map(
        body, mesh=mesh, in_specs=placed, out_specs=P(("ox", "oy"), None, None), check_vma=False
    )
```

```python
import functools

import jax
import jax.numpy as jnp
from jax import lax
from jax.experimental import pallas as pl
from jax.experimental.pallas import tpu as pltpu
from jax.sharding import PartitionSpec as P

BLOCK = 128
LANES = 128
PACK = 16
AXES = ("ox", "oy")


def flatten_kernel(field_ref, *rest):
    out_ref, slabs, wide, rows32, sem = rest[-5:]
    pieces, columns, _, channels = slabs.shape
    halves = channels // LANES
    pitch = wide.shape[1] // columns
    margin = (out_ref.shape[0] - pieces * columns) // 2

    def fetch(piece):
        source = field_ref.at[:, pl.ds(pl.multiple_of(piece * PACK, PACK), PACK), :]
        return pltpu.make_async_copy(source, slabs.at[piece], sem.at[piece])

    @pl.loop(0, pieces)
    def _(piece):
        fetch(piece).start()

    @pl.loop(0, pieces)
    def _(piece):
        fetch(piece).wait()

        @pl.loop(0, columns, unroll=4)
        def _(column):
            value = slabs[piece, column].astype(jnp.float32)
            for half in range(halves):
                part = value[:, half * LANES : (half + 1) * LANES]
                wide[half, pl.ds(column * pitch, PACK), :] = part

        for row in range(PACK):
            for half in range(halves):
                picked = wide[half, pl.ds(row, columns, stride=pitch), :]
                rows32[half, pl.ds(row * columns, columns), :] = picked

        @pl.loop(0, columns, unroll=4)
        def _(step):
            base = pl.multiple_of(step * PACK, PACK)
            parts = [rows32[half, pl.ds(base, PACK), :] for half in range(halves)]
            out_ref[margin + piece * columns + step] = jnp.concatenate(parts, 1).astype(out_ref.dtype)


def flatten_cells(field, before):
    columns, rows, channels = field.shape
    pieces, halves = rows // PACK, channels // LANES
    margin = columns // PACK + 1
    return pl.pallas_call(
        flatten_kernel,
        out_shape=jax.ShapeDtypeStruct((pieces * columns + 2 * margin, PACK, channels), field.dtype),
        in_specs=[pl.BlockSpec(memory_space=pltpu.HBM)] + [pl.BlockSpec(memory_space=pl.ANY)] * len(before),
        out_specs=pl.BlockSpec(memory_space=pltpu.VMEM),
        scratch_shapes=[
            pltpu.VMEM((pieces, columns, PACK, channels), field.dtype),
            pltpu.VMEM((halves, columns * (PACK + 1), LANES), jnp.float32),
            pltpu.VMEM((halves, columns * PACK, LANES), jnp.float32),
            pltpu.SemaphoreType.DMA((pieces,)),
        ],
        compiler_params=pltpu.CompilerParams(vmem_limit_bytes=24 << 20),
        cost_estimate=pl.CostEstimate(flops=0, bytes_accessed=24 << 20, transcendentals=0),
        name="flatten",
    )(field, *before)


def smooth_kernel(masks, columns, rows, cap, asked, place, cells, coeff_ref, east_ref, west_ref, inner_ref, outer_ref, *rest):
    rest = rest[len(rest) - len(masks) - 8 :]
    outs = rest[: len(masks)]
    mid32, top32, bot32, rim_e, rim_w, rim_s, rim_n, made = rest[len(masks) :]
    channels = east_ref.shape[1]
    halves = channels // LANES
    me = place[0]
    up, shift = columns // PACK, columns % PACK
    margin = up + 1
    parts = ((-1, mid32), (up, top32), (-up - 1, bot32))

    def request(i):
        mask = masks[0]
        for j in range(1, len(masks)):
            mask = jnp.where(i // cap == j, masks[j], mask)
        return asked[me ^ mask, i % cap]

    odd, at_top = place[1] == 1, place[2] == 1
    for half in range(halves):
        lanes = pl.ds(half * LANES, LANES)
        rim_e[half] = east_ref[:, lanes].astype(jnp.float32)
        rim_w[half] = west_ref[:, lanes].astype(jnp.float32)
        inner, outer = inner_ref[:, lanes], outer_ref[:, lanes]
        rim_s[half] = jnp.where(odd, inner.astype(jnp.float32), outer.astype(jnp.float32))
        rim_n[half] = jnp.where(odd, outer.astype(jnp.float32), inner.astype(jnp.float32))

    @pl.when(at_top)
    def _():
        for half in range(halves):

            @pl.loop(0, columns // 2)
            def _(i):
                left = rim_n[half, pl.ds(i, 1), :]
                right = rim_n[half, pl.ds(columns - 1 - i, 1), :]
                rim_n[half, pl.ds(i, 1), :] = right
                rim_n[half, pl.ds(columns - 1 - i, 1), :] = left

    cell = lax.broadcasted_iota(jnp.int32, (BLOCK, LANES), 0)

    @pl.loop(0, len(masks) * cap)
    def _(i):
        block = request(i)
        for offset, wide in parts:
            for step in range(wide.shape[1] // PACK):
                value = cells[margin + block * (BLOCK // PACK) + offset + step].astype(jnp.float32)
                for half in range(halves):
                    part = value[:, half * LANES : (half + 1) * LANES]
                    wide[half, step * PACK : (step + 1) * PACK, :] = part
        total = rows * columns // BLOCK
        for n in range(pl.cdiv(columns, BLOCK)):
            low = n * BLOCK
            size = min(BLOCK, columns - low)

            @pl.when(block == n)
            def _():
                for half in range(halves):
                    bot32[half, PACK - shift : PACK - shift + size, :] = rim_s[half, low : low + size, :]

            begin = (total - 1 - n) * BLOCK - (rows - 1) * columns
            skip = max(0, -begin)

            @pl.when(block == total - 1 - n)
            def _():
                for half in range(halves):
                    top32[half, shift + skip : shift + BLOCK, :] = rim_n[half, begin + skip : begin + BLOCK, :]

        row = (block * BLOCK + columns - 1) // columns
        edge = row * columns - block * BLOCK
        row_w = jnp.minimum(row, rows - 1)
        row_e = jnp.maximum(row - 1, 0)
        scale = jnp.broadcast_to(coeff_ref[pl.ds(block, 1), :], (BLOCK, LANES)).T
        for half in range(halves):
            centre = mid32[half, PACK : PACK + BLOCK, :]
            east = mid32[half, PACK + 1 : PACK + 1 + BLOCK, :]
            west = mid32[half, PACK - 1 : PACK - 1 + BLOCK, :]
            north = top32[half, shift : shift + BLOCK, :]
            south = bot32[half, PACK - shift : PACK - shift + BLOCK, :]
            west = jnp.where(cell == edge, rim_w[half, pl.ds(row_w, 1), :], west)
            east = jnp.where(cell == edge - 1, rim_e[half, pl.ds(row_e, 1), :], east)
            beside = north + south + east + west
            value = centre + scale * (beside - 4.0 * centre)
            made[i, :, half * LANES : (half + 1) * LANES] = value.astype(made.dtype)

    for j, out in enumerate(outs):
        out[...] = made[j * cap : (j + 1) * cap]


def smooth_blocks(masks, asked, place, cells, coeff, east, west, inner, outer, before):
    channels = cells.shape[2]
    cap = asked.shape[1]
    count = len(masks) * cap
    run = BLOCK // PACK
    rows, columns = east.shape[0], inner.shape[0]
    anywhere = pl.BlockSpec(memory_space=pl.ANY)
    inside = pl.BlockSpec(memory_space=pltpu.VMEM)
    steps = (run + 2, run + 1, run + 1)
    halves = channels // LANES
    return pl.pallas_call(
        functools.partial(smooth_kernel, masks, columns, rows, cap),
        out_shape=[jax.ShapeDtypeStruct((cap, BLOCK, channels), cells.dtype)] * len(masks),
        grid_spec=pltpu.PrefetchScalarGridSpec(
            num_scalar_prefetch=2,
            grid=(),
            in_specs=[inside] * 6 + [anywhere] * len(before),
            out_specs=[inside] * len(masks),
            scratch_shapes=[pltpu.VMEM((halves, n * PACK, LANES), jnp.float32) for n in steps]
            + [pltpu.VMEM((halves, n, LANES), jnp.float32) for n in (rows, rows, columns, columns)]
            + [
                pltpu.VMEM((count, BLOCK, channels), cells.dtype),
            ],
        ),
        cost_estimate=pl.CostEstimate(
            flops=count * BLOCK * channels * 8,
            bytes_accessed=count * BLOCK * channels * 10,
            transcendentals=0,
        ),
        compiler_params=pltpu.CompilerParams(vmem_limit_bytes=12 << 20),
        name="smooth",
    )(asked, place, cells, coeff, east, west, inner, outer, *before)


def remap_kernel(masks, cap, slots, last, column, table, weights, *rest):
    arrived = rest[: len(masks)]
    rest = rest[len(masks) :]
    start_ref, ready = rest[:2] if last else (None, None)
    out_ref, *rest = rest[2 if last else 0 :]
    later = None if last else rest.pop(0)
    blocks, held, weight_sem, *made = rest
    dests, terms = held.shape[:2]
    me = table[0, table.shape[1] - 1]
    first = min(4, terms)
    bounds = [n for n in (8,) if n < terms] + [terms]

    def number(dest):
        return table[dest, column + terms]

    def used(dest):
        size = jnp.int32(first)
        low = first
        for bound in bounds:
            size = jnp.where(number(dest) > low, bound, size)
            low = bound
        return size

    def weight_copy(dest, place):
        term = table[dest, column + place] >> 16
        return pltpu.make_async_copy(weights.at[dest, term], held.at[dest, place], weight_sem.at[dest])

    begin = first if last else 0

    @pl.loop(0, dests)
    def _(dest):
        @pl.loop(begin, used(dest))
        def _(place):
            weight_copy(dest, place).start()

    def later_copy(dest, place):
        term = table[dest, column + terms + 1 + place] >> 16
        return pltpu.make_async_copy(weights.at[dest, term], later.at[dest, place], made[0].at[0])

    if not last:

        @pl.loop(0, dests)
        def _(dest):
            for place in range(first):
                later_copy(dest, place).start()

    blocks[slots] = jnp.zeros(blocks.shape[1:], blocks.dtype)
    for mask, ref in zip(masks, arrived):
        for c in range(cap):
            blocks[(me ^ mask) * cap + c] = ref[c]

    def product(dest, low, high):
        left = [ready[dest, g] if last and g < first else held[dest, g] for g in range(low, high)]
        right = [blocks[table[dest, column + g] & 65535] for g in range(low, high)]
        return jnp.dot(
            jnp.concatenate(left, 1), jnp.concatenate(right, 0), preferred_element_type=jnp.float32
        )

    def store(dest, value):
        if last:
            made[0][dest] = value.astype(made[0].dtype)
        else:
            out_ref[dest] = value

    def send(dest):
        return pltpu.make_async_copy(made[0].at[dest], out_ref.at[dest], made[1].at[0])

    together = 4 if dests % 4 == 0 else 1

    @pl.loop(0, dests // together)
    def _(group):
        for u in range(together):

            @pl.loop(begin, used(group * together + u))
            def _(place):
                weight_copy(group * together + u, place).wait()

        for u in range(together):
            dest = group * together + u
            value = product(dest, 0, first)
            store(dest, start_ref[dest] + value if last else value)
        for u in range(together):
            dest = group * together + u
            low = first
            for bound in bounds:

                @pl.when((number(dest) > low) & (number(dest) <= bound) if last else number(dest) > low)
                def _():
                    if last:
                        store(dest, start_ref[dest] + product(dest, 0, bound))
                    else:
                        store(dest, out_ref[dest] + product(dest, low, bound))

                low = bound
        if last:
            for u in range(together):
                send(group * together + u).start()

    @pl.loop(0, dests)
    def _(dest):
        if last:
            send(dest).wait()
        else:
            for place in range(first):
                later_copy(dest, place).wait()


def remap(masks, cap, slots, column, table, weights, arrived, start, dtype):
    dests, terms = weights.shape[:2]
    channels = arrived[0].shape[2]
    last = start is not None
    anywhere = pl.BlockSpec(memory_space=pl.ANY)
    inside = pl.BlockSpec(memory_space=pltpu.VMEM)
    shape = (dests, BLOCK, channels)
    result = jax.ShapeDtypeStruct(shape, dtype)
    ready = (dests, min(4, terms), BLOCK, BLOCK)
    return pl.pallas_call(
        functools.partial(remap_kernel, masks, cap, slots, last, column),
        out_shape=result if last else (result, jax.ShapeDtypeStruct(ready, weights.dtype)),
        grid_spec=pltpu.PrefetchScalarGridSpec(
            num_scalar_prefetch=1,
            grid=(),
            in_specs=[anywhere] + [inside] * (len(masks) + 2 * last),
            out_specs=anywhere if last else (inside, inside),
            scratch_shapes=[
                pltpu.VMEM((slots + 1, BLOCK, channels), arrived[0].dtype),
                pltpu.VMEM((dests, terms, BLOCK, BLOCK), weights.dtype),
                pltpu.SemaphoreType.DMA((dests,)),
            ]
            + ([pltpu.VMEM(shape, dtype)] if last else [])
            + [pltpu.SemaphoreType.DMA((1,))],
        ),
        compiler_params=pltpu.CompilerParams(vmem_limit_bytes=40 << 20),
        cost_estimate=pl.CostEstimate(
            flops=dests * terms * BLOCK * BLOCK * channels,
            bytes_accessed=weights.size,
            transcendentals=0,
        ),
        name="remap_last" if last else "remap_early",
    )(table, weights, *arrived, *(start if last else []))


def term_table(slot_ids, chosen, slots):
    terms = slot_ids.shape[1]
    index = jnp.arange(terms, dtype=jnp.int32)
    key = jnp.where(chosen, index[None, :], index[None, :] + terms)
    rank = jnp.sum(key[:, None, :] < key[:, :, None], axis=2)
    entry = index[None, :] * 65536 + jnp.where(chosen, slot_ids, slots)
    hit = rank[:, :, None] == index[None, None, :]
    ordered = jnp.sum(jnp.where(hit, entry[:, :, None], 0), axis=1)
    number = jnp.sum(chosen, axis=1, dtype=jnp.int32)[:, None]
    return [ordered, number]


def body(ocean_state, diffusivity, requests, slot_ids, counts, remap_weights):
    n_ox, n_oy = lax.axis_size("ox"), lax.axis_size("oy")
    devices = n_ox * n_oy
    rows, _, _ = ocean_state.shape
    cap = requests.shape[2]
    slots = devices * cap
    ox, oy = lax.axis_index("ox"), lax.axis_index("oy")
    me = (ox * n_oy + oy).astype(jnp.int32)
    assert devices & (devices - 1) == 0 and n_oy % 2 == 0 and rows % PACK == 0

    asked = lax.all_to_all(requests[0], AXES, split_axis=0, concat_axis=0, tiled=True)
    field = jnp.transpose(ocean_state, (1, 0, 2))
    held_field = pltpu.with_memory_space_constraint(field, pltpu.HBM)
    ring = [(i, (i + 1) % n_ox) for i in range(n_ox)]
    west = lax.ppermute(field[-1], "ox", ring)
    east = lax.ppermute(field[0], "ox", [(j, i) for i, j in ring])
    first_row, last_row = ocean_state[0], ocean_state[-1]
    odd = oy % 2 == 1
    top = n_oy - 1
    pairs = [(ox_ * n_oy + i, ox_ * n_oy + (i ^ 1)) for ox_ in range(n_ox) for i in range(n_oy)]
    inner = lax.ppermute(jnp.where(odd, first_row, last_row), AXES, pairs)
    pairs = [(i * n_oy + top, (n_ox - 1 - i) * n_oy + top) for i in range(n_ox)]
    for i in range(1, top, 2):
        for ox_ in range(n_ox):
            base = ox_ * n_oy + i
            pairs += [(base, base + 1), (base + 1, base)]
    outer = lax.ppermute(jnp.where(odd, last_row, first_row), AXES, pairs)

    coeff = diffusivity.reshape(-1, BLOCK)
    cells = flatten_cells(held_field, (coeff, asked))
    place = jnp.stack([me, odd.astype(jnp.int32), (oy == top).astype(jnp.int32)])

    half = n_oy // 2
    across = [m for m in range(devices) if m & half]
    beside = [m for m in range(devices) if not m & half]
    lead = 4
    order = across[:lead]
    for i, m in enumerate(beside[1:] + [beside[0]]):
        order += [m] + across[lead + i : lead + i + 1]
    late = across[-max(1, min(7, len(across) * 7 // 16)) :]
    order = [m for m in order if m not in late] + late
    groups = [order[:lead]] + [order[i : i + 10] for i in range(lead, devices, 10)]
    arrived, before = {}, []
    for number, group in enumerate(groups):
        made = smooth_blocks(tuple(group), asked, place, cells, coeff, east, west, inner, outer, before)
        if number == len(groups) - 1:
            slot_ids, counts, made = lax.optimization_barrier((slot_ids, counts, made))
        before = made[:1]
        for m, blocks in zip(group, made):
            pairs = [(i, i ^ m) for i in range(devices)]
            arrived[m] = lax.ppermute(blocks, AXES, pairs) if m else blocks

    term_total = slot_ids.shape[1]
    live = jnp.arange(term_total, dtype=jnp.int32)[None, :] < counts[:, None]
    offset = me ^ (slot_ids // cap)
    is_late = functools.reduce(jnp.logical_or, [offset == m for m in late])
    early = [m for m in order if m not in late]
    parts = term_table(slot_ids, live & ~is_late, slots) + term_table(slot_ids, live & is_late, slots)
    table = jnp.concatenate(parts + [jnp.full_like(parts[1], me)], axis=1)
    partial = remap(tuple(early), cap, slots, 0, table, remap_weights, [arrived[m] for m in early], None, jnp.float32)
    return remap(
        tuple(late), cap, slots, term_total + 1, table, remap_weights, [arrived[m] for m in late], partial, jnp.bfloat16
    )


def solution(mesh):
    placed = (
        P("oy", "ox", None),
        P("oy", "ox"),
        P(("ox", "oy"), None, None),
        P(("ox", "oy"), None),
        P(("ox", "oy")),
        P(("ox", "oy"), None, None, None),
    )
    return jax.shard_map(body, mesh=mesh, in_specs=placed, out_specs=P(("ox", "oy"), None, None), check_vma=False)
```

```python
import functools

import jax
import jax.numpy as jnp
from jax import lax
from jax.experimental import pallas as pl
from jax.experimental.pallas import tpu as pltpu
from jax.sharding import PartitionSpec as P

BLOCK = 128
LANES = 128
PACK = 16
AXES = ("ox", "oy")


def flatten_kernel(field_ref, *rest):
    out_ref, slabs, wide, rows32, sem = rest[-5:]
    pieces, columns, _, channels = slabs.shape
    halves = channels // LANES
    pitch = wide.shape[1] // columns
    margin = (out_ref.shape[0] - pieces * columns) // 2

    def fetch(piece):
        source = field_ref.at[:, pl.ds(pl.multiple_of(piece * PACK, PACK), PACK), :]
        return pltpu.make_async_copy(source, slabs.at[piece], sem.at[piece])

    @pl.loop(0, pieces)
    def _(piece):
        fetch(piece).start()

    @pl.loop(0, pieces)
    def _(piece):
        fetch(piece).wait()

        @pl.loop(0, columns, unroll=4)
        def _(column):
            value = slabs[piece, column].astype(jnp.float32)
            for half in range(halves):
                part = value[:, half * LANES : (half + 1) * LANES]
                wide[half, pl.ds(column * pitch, PACK), :] = part

        for row in range(PACK):
            for half in range(halves):
                picked = wide[half, pl.ds(row, columns, stride=pitch), :]
                rows32[half, pl.ds(row * columns, columns), :] = picked

        @pl.loop(0, columns, unroll=4)
        def _(step):
            base = pl.multiple_of(step * PACK, PACK)
            parts = [rows32[half, pl.ds(base, PACK), :] for half in range(halves)]
            out_ref[margin + piece * columns + step] = jnp.concatenate(parts, 1).astype(out_ref.dtype)


def flatten_cells(field, before):
    columns, rows, channels = field.shape
    pieces, halves = rows // PACK, channels // LANES
    margin = columns // PACK + 1
    return pl.pallas_call(
        flatten_kernel,
        out_shape=jax.ShapeDtypeStruct((pieces * columns + 2 * margin, PACK, channels), field.dtype),
        in_specs=[pl.BlockSpec(memory_space=pltpu.HBM)] + [pl.BlockSpec(memory_space=pl.ANY)] * len(before),
        out_specs=pl.BlockSpec(memory_space=pltpu.VMEM),
        scratch_shapes=[
            pltpu.VMEM((pieces, columns, PACK, channels), field.dtype),
            pltpu.VMEM((halves, columns * (PACK + 1), LANES), jnp.float32),
            pltpu.VMEM((halves, columns * PACK, LANES), jnp.float32),
            pltpu.SemaphoreType.DMA((pieces,)),
        ],
        compiler_params=pltpu.CompilerParams(vmem_limit_bytes=24 << 20),
        cost_estimate=pl.CostEstimate(flops=0, bytes_accessed=24 << 20, transcendentals=0),
        name="flatten",
    )(field, *before)


def smooth_kernel(masks, columns, rows, cap, asked, place, cells, coeff_ref, east_ref, west_ref, inner_ref, outer_ref, *rest):
    rest = rest[len(rest) - len(masks) - 8 :]
    outs = rest[: len(masks)]
    mid32, top32, bot32, rim_e, rim_w, rim_s, rim_n, made = rest[len(masks) :]
    channels = east_ref.shape[1]
    halves = channels // LANES
    me = place[0]
    up, shift = columns // PACK, columns % PACK
    margin = up + 1
    parts = ((-1, mid32), (up, top32), (-up - 1, bot32))

    def request(i):
        mask = masks[0]
        for j in range(1, len(masks)):
            mask = jnp.where(i // cap == j, masks[j], mask)
        return asked[me ^ mask, i % cap]

    odd, at_top = place[1] == 1, place[2] == 1
    for half in range(halves):
        lanes = pl.ds(half * LANES, LANES)
        rim_e[half] = east_ref[:, lanes].astype(jnp.float32)
        rim_w[half] = west_ref[:, lanes].astype(jnp.float32)
        inner, outer = inner_ref[:, lanes], outer_ref[:, lanes]
        rim_s[half] = jnp.where(odd, inner.astype(jnp.float32), outer.astype(jnp.float32))
        rim_n[half] = jnp.where(odd, outer.astype(jnp.float32), inner.astype(jnp.float32))

    @pl.when(at_top)
    def _():
        for half in range(halves):

            @pl.loop(0, columns // 2)
            def _(i):
                left = rim_n[half, pl.ds(i, 1), :]
                right = rim_n[half, pl.ds(columns - 1 - i, 1), :]
                rim_n[half, pl.ds(i, 1), :] = right
                rim_n[half, pl.ds(columns - 1 - i, 1), :] = left

    cell = lax.broadcasted_iota(jnp.int32, (BLOCK, LANES), 0)

    @pl.loop(0, len(masks) * cap)
    def _(i):
        block = request(i)
        for offset, wide in parts:
            for step in range(wide.shape[1] // PACK):
                value = cells[margin + block * (BLOCK // PACK) + offset + step].astype(jnp.float32)
                for half in range(halves):
                    part = value[:, half * LANES : (half + 1) * LANES]
                    wide[half, step * PACK : (step + 1) * PACK, :] = part
        total = rows * columns // BLOCK
        for n in range(pl.cdiv(columns, BLOCK)):
            low = n * BLOCK
            size = min(BLOCK, columns - low)

            @pl.when(block == n)
            def _():
                for half in range(halves):
                    bot32[half, PACK - shift : PACK - shift + size, :] = rim_s[half, low : low + size, :]

            begin = (total - 1 - n) * BLOCK - (rows - 1) * columns
            skip = max(0, -begin)

            @pl.when(block == total - 1 - n)
            def _():
                for half in range(halves):
                    top32[half, shift + skip : shift + BLOCK, :] = rim_n[half, begin + skip : begin + BLOCK, :]

        row = (block * BLOCK + columns - 1) // columns
        edge = row * columns - block * BLOCK
        row_w = jnp.minimum(row, rows - 1)
        row_e = jnp.maximum(row - 1, 0)
        scale = jnp.broadcast_to(coeff_ref[pl.ds(block, 1), :], (BLOCK, LANES)).T
        for half in range(halves):
            centre = mid32[half, PACK : PACK + BLOCK, :]
            east = mid32[half, PACK + 1 : PACK + 1 + BLOCK, :]
            west = mid32[half, PACK - 1 : PACK - 1 + BLOCK, :]
            north = top32[half, shift : shift + BLOCK, :]
            south = bot32[half, PACK - shift : PACK - shift + BLOCK, :]
            west = jnp.where(cell == edge, rim_w[half, pl.ds(row_w, 1), :], west)
            east = jnp.where(cell == edge - 1, rim_e[half, pl.ds(row_e, 1), :], east)
            beside = north + south + east + west
            value = centre + scale * (beside - 4.0 * centre)
            made[i, :, half * LANES : (half + 1) * LANES] = value.astype(made.dtype)

    for j, out in enumerate(outs):
        out[...] = made[j * cap : (j + 1) * cap]


def smooth_blocks(masks, asked, place, cells, coeff, east, west, inner, outer, before):
    channels = cells.shape[2]
    cap = asked.shape[1]
    count = len(masks) * cap
    run = BLOCK // PACK
    rows, columns = east.shape[0], inner.shape[0]
    anywhere = pl.BlockSpec(memory_space=pl.ANY)
    inside = pl.BlockSpec(memory_space=pltpu.VMEM)
    steps = (run + 2, run + 1, run + 1)
    halves = channels // LANES
    return pl.pallas_call(
        functools.partial(smooth_kernel, masks, columns, rows, cap),
        out_shape=[jax.ShapeDtypeStruct((cap, BLOCK, channels), cells.dtype)] * len(masks),
        grid_spec=pltpu.PrefetchScalarGridSpec(
            num_scalar_prefetch=2,
            grid=(),
            in_specs=[inside] * 6 + [anywhere] * len(before),
            out_specs=[inside] * len(masks),
            scratch_shapes=[pltpu.VMEM((halves, n * PACK, LANES), jnp.float32) for n in steps]
            + [pltpu.VMEM((halves, n, LANES), jnp.float32) for n in (rows, rows, columns, columns)]
            + [
                pltpu.VMEM((count, BLOCK, channels), cells.dtype),
            ],
        ),
        cost_estimate=pl.CostEstimate(
            flops=count * BLOCK * channels * 8,
            bytes_accessed=count * BLOCK * channels * 10,
            transcendentals=0,
        ),
        compiler_params=pltpu.CompilerParams(vmem_limit_bytes=12 << 20),
        name="smooth",
    )(asked, place, cells, coeff, east, west, inner, outer, *before)


def remap_kernel(masks, cap, slots, last, column, table, weights, *rest):
    arrived = rest[: len(masks)]
    rest = rest[len(masks) :]
    start_ref, ready = rest[:2] if last else (None, None)
    out_ref, *rest = rest[2 if last else 0 :]
    later = None if last else rest.pop(0)
    blocks, held, weight_sem, *made = rest
    dests, terms = held.shape[:2]
    me = table[0, table.shape[1] - 1]
    stock = min(4, terms)
    first = min(2, terms) if last else stock
    bounds = [n for n in ((4, 8) if last else (8,)) if n < terms] + [terms]

    def number(dest):
        return table[dest, column + terms]

    def used(dest):
        size = jnp.int32(first)
        low = first
        for bound in bounds:
            size = jnp.where(number(dest) > low, bound, size)
            low = bound
        return size

    def weight_copy(dest, place):
        term = table[dest, column + place] >> 16
        return pltpu.make_async_copy(weights.at[dest, term], held.at[dest, place], weight_sem.at[dest])

    begin = stock if last else 0

    @pl.when(table[0, table.shape[1] - 2] > begin if last else table[0, table.shape[1] - 2] >= 0)
    def _():
        @pl.loop(0, dests)
        def _(dest):
            @pl.loop(begin, used(dest))
            def _(place):
                weight_copy(dest, place).start()

    def later_copy(dest, place):
        term = table[dest, column + terms + 1 + place] >> 16
        return pltpu.make_async_copy(weights.at[dest, term], later.at[dest, place], made[0].at[0])

    if not last:

        @pl.loop(0, dests)
        def _(dest):
            for place in range(stock):
                later_copy(dest, place).start()

    blocks[slots] = jnp.zeros(blocks.shape[1:], blocks.dtype)
    for mask, ref in zip(masks, arrived):
        for c in range(cap):
            blocks[(me ^ mask) * cap + c] = ref[c]

    def product(dest, low, high):
        left = [ready[dest, g] if last and g < stock else held[dest, g] for g in range(low, high)]
        right = [blocks[table[dest, column + g] & 65535] for g in range(low, high)]
        return jnp.dot(
            jnp.concatenate(left, 1), jnp.concatenate(right, 0), preferred_element_type=jnp.float32
        )

    def store(dest, value):
        if last:
            made[0][dest] = value.astype(made[0].dtype)
        else:
            out_ref[dest] = value

    def send(dest):
        return pltpu.make_async_copy(made[0].at[dest], out_ref.at[dest], made[1].at[0])

    together = 4 if dests % 4 == 0 else 1

    @pl.loop(0, dests // together)
    def _(group):
        def wait():
            for u in range(together):

                @pl.loop(begin, used(group * together + u))
                def _(place):
                    weight_copy(group * together + u, place).wait()

        def more():
            for u in range(together):
                dest = group * together + u
                low = first
                for bound in bounds:

                    @pl.when((number(dest) > low) & (number(dest) <= bound) if last else number(dest) > low)
                    def _():
                        if last:
                            store(dest, start_ref[dest] + product(dest, 0, bound))
                        else:
                            store(dest, out_ref[dest] + product(dest, low, bound))

                    low = bound

        if not last:
            wait()
        for u in range(together):
            dest = group * together + u
            value = product(dest, 0, first)
            store(dest, start_ref[dest] + value if last else value)
        most = number(group * together)
        for u in range(1, together):
            most = jnp.maximum(most, number(group * together + u))

        @pl.when(most > first)
        def _():
            if last:
                wait()
            more()

        if last:
            for u in range(together):
                send(group * together + u).start()

    @pl.loop(0, dests)
    def _(dest):
        if last:
            send(dest).wait()
        else:
            for place in range(stock):
                later_copy(dest, place).wait()


def remap(masks, cap, slots, column, table, weights, arrived, start, dtype):
    dests, terms = weights.shape[:2]
    channels = arrived[0].shape[2]
    last = start is not None
    anywhere = pl.BlockSpec(memory_space=pl.ANY)
    inside = pl.BlockSpec(memory_space=pltpu.VMEM)
    shape = (dests, BLOCK, channels)
    result = jax.ShapeDtypeStruct(shape, dtype)
    ready = (dests, min(4, terms), BLOCK, BLOCK)
    return pl.pallas_call(
        functools.partial(remap_kernel, masks, cap, slots, last, column),
        out_shape=result if last else (result, jax.ShapeDtypeStruct(ready, weights.dtype)),
        grid_spec=pltpu.PrefetchScalarGridSpec(
            num_scalar_prefetch=1,
            grid=(),
            in_specs=[anywhere] + [inside] * (len(masks) + 2 * last),
            out_specs=anywhere if last else (inside, inside),
            scratch_shapes=[
                pltpu.VMEM((slots + 1, BLOCK, channels), arrived[0].dtype),
                pltpu.VMEM((dests, terms, BLOCK, BLOCK), weights.dtype),
                pltpu.SemaphoreType.DMA((dests,)),
            ]
            + ([pltpu.VMEM(shape, dtype)] if last else [])
            + [pltpu.SemaphoreType.DMA((1,))],
        ),
        compiler_params=pltpu.CompilerParams(vmem_limit_bytes=40 << 20),
        cost_estimate=pl.CostEstimate(
            flops=dests * terms * BLOCK * BLOCK * channels,
            bytes_accessed=weights.size,
            transcendentals=0,
        ),
        name="remap_last" if last else "remap_early",
    )(table, weights, *arrived, *(start if last else []))


def term_table(slot_ids, chosen, slots):
    terms = slot_ids.shape[1]
    index = jnp.arange(terms, dtype=jnp.int32)
    key = jnp.where(chosen, index[None, :], index[None, :] + terms)
    rank = jnp.sum(key[:, None, :] < key[:, :, None], axis=2)
    entry = index[None, :] * 65536 + jnp.where(chosen, slot_ids, slots)
    hit = rank[:, :, None] == index[None, None, :]
    ordered = jnp.sum(jnp.where(hit, entry[:, :, None], 0), axis=1)
    number = jnp.sum(chosen, axis=1, dtype=jnp.int32)[:, None]
    return [ordered, number]


def body(ocean_state, diffusivity, requests, slot_ids, counts, remap_weights):
    n_ox, n_oy = lax.axis_size("ox"), lax.axis_size("oy")
    devices = n_ox * n_oy
    rows, _, _ = ocean_state.shape
    cap = requests.shape[2]
    slots = devices * cap
    ox, oy = lax.axis_index("ox"), lax.axis_index("oy")
    me = (ox * n_oy + oy).astype(jnp.int32)
    assert devices & (devices - 1) == 0 and n_oy % 2 == 0 and rows % PACK == 0

    asked = lax.all_to_all(requests[0], AXES, split_axis=0, concat_axis=0, tiled=True)
    field = jnp.transpose(ocean_state, (1, 0, 2))
    held_field = pltpu.with_memory_space_constraint(field, pltpu.HBM)
    ring = [(i, (i + 1) % n_ox) for i in range(n_ox)]
    west = lax.ppermute(field[-1], "ox", ring)
    east = lax.ppermute(field[0], "ox", [(j, i) for i, j in ring])
    first_row, last_row = ocean_state[0], ocean_state[-1]
    odd = oy % 2 == 1
    top = n_oy - 1
    pairs = [(ox_ * n_oy + i, ox_ * n_oy + (i ^ 1)) for ox_ in range(n_ox) for i in range(n_oy)]
    inner = lax.ppermute(jnp.where(odd, first_row, last_row), AXES, pairs)
    pairs = [(i * n_oy + top, (n_ox - 1 - i) * n_oy + top) for i in range(n_ox)]
    for i in range(1, top, 2):
        for ox_ in range(n_ox):
            base = ox_ * n_oy + i
            pairs += [(base, base + 1), (base + 1, base)]
    outer = lax.ppermute(jnp.where(odd, last_row, first_row), AXES, pairs)

    coeff = diffusivity.reshape(-1, BLOCK)
    cells = flatten_cells(held_field, (coeff, asked))
    place = jnp.stack([me, odd.astype(jnp.int32), (oy == top).astype(jnp.int32)])

    half = n_oy // 2
    across = [m for m in range(devices) if m & half]
    beside = [m for m in range(devices) if not m & half]
    lead = min(3, len(across))
    order = across[:lead]
    for i, m in enumerate(beside[1:] + [beside[0]]):
        order += [m] + across[lead + i : lead + i + 1]
    late = across[-max(1, min(7, len(across) * 7 // 16)) :]
    order = [m for m in order if m not in late] + late
    groups = [order[:lead], order[lead : lead + 8]]
    groups += [order[i : i + 10] for i in range(lead + 8, devices, 10)]
    arrived, before = {}, []
    for number, group in enumerate(groups):
        made = smooth_blocks(tuple(group), asked, place, cells, coeff, east, west, inner, outer, before)
        if number == len(groups) - 1:
            slot_ids, counts, made = lax.optimization_barrier((slot_ids, counts, made))
        before = made[:1]
        for m, blocks in zip(group, made):
            pairs = [(i, i ^ m) for i in range(devices)]
            arrived[m] = lax.ppermute(blocks, AXES, pairs) if m else blocks

    term_total = slot_ids.shape[1]
    live = jnp.arange(term_total, dtype=jnp.int32)[None, :] < counts[:, None]
    offset = me ^ (slot_ids // cap)
    is_late = functools.reduce(jnp.logical_or, [offset == m for m in late])
    early = [m for m in order if m not in late]
    parts = term_table(slot_ids, live & ~is_late, slots) + term_table(slot_ids, live & is_late, slots)
    most = jnp.full_like(parts[1], jnp.max(parts[3]))
    table = jnp.concatenate(parts + [most, jnp.full_like(parts[1], me)], axis=1)
    partial = remap(tuple(early), cap, slots, 0, table, remap_weights, [arrived[m] for m in early], None, jnp.float32)
    return remap(
        tuple(late), cap, slots, term_total + 1, table, remap_weights, [arrived[m] for m in late], partial, jnp.bfloat16
    )


def solution(mesh):
    placed = (
        P("oy", "ox", None),
        P("oy", "ox"),
        P(("ox", "oy"), None, None),
        P(("ox", "oy"), None),
        P(("ox", "oy")),
        P(("ox", "oy"), None, None, None),
    )
    return jax.shard_map(body, mesh=mesh, in_specs=placed, out_specs=P(("ox", "oy"), None, None), check_vma=False)
```
